32 devices in a mesh: dp: 4 (over y, core), expert: 8 (over z, x).
Axes of the slice: x: 2, y: 2, z: 4, core: 2. Of those that a mesh axis runs over, the one named last changes fastest.
Arguments:
- tokens: bfloat16 [1024, 7168], P('expert', 'dp'), may hold values from -6 to 6
- routes: int32 [1024, 8], P('expert'), may hold values from 0 to 31, all different within a row; in each aligned block of 128 rows (0 to 127, 128 to 255, ...) at most 64 rows name the same one
- route_weight: float32 [1024, 8], P('expert'), may hold values from 0.1 to 1
- gate_first: bfloat16 [32, 64, 112, 32], P('expert', 'dp'), may hold values from -0.5 to 0.5
- up_first: bfloat16 [32, 64, 112, 32], P('expert', 'dp'), may hold values from -0.5 to 0.5
- gate_second: bfloat16 [32, 32, 64, 64], P('expert', 'dp'), may hold values from -0.75 to 0.75
- up_second: bfloat16 [32, 32, 64, 64], P('expert', 'dp'), may hold values from -0.75 to 0.75
- down_first: bfloat16 [32, 32, 64, 64], P('expert', 'dp'), may hold values from -0.75 to 0.75
- down_second: bfloat16 [32, 64, 32, 112], P('expert', 'dp'), may hold values from -1 to 1
Outputs:
- moe_output: bfloat16 [1024, 7168], P('expert', 'dp')
- expert_load: float32 [32], P('expert')
The draws below stay inside these ranges and needn't reach their ends.
Inputs may be any that keep to these rules, and one draw needn't show every extreme that they name: `routes`: each row names 8 different experts. Within each device's aligned block of 128 rows no expert is named by more than 64 rows, and in some block an expert is named by exactly 64 rows.
All inputs are finite; a program needn't handle non-finite values.
Results may differ from the reference program's by a relative error of at most 0.0076.
Values may be sent and summed in bfloat16 or wider, within the bound.
A program may use at most 64 MiB of HBM per device.

```python
import math
import jax
import jax.numpy as jnp
import numpy as np
from jax import lax

D = 7168
TOP = 8
BLOCKS = 64
TOK_DEV = 128
EXPERTS = 32
TOKENS = 1024
CAP = 64
BW = 112
RANK = 32
N_EXPERT = 8


def block_scale(rng, shape, pieces, smallest, top_value):
    def one(axis_at, parts):
        heights = jax.random.uniform(jax.random.fold_in(jax.random.fold_in(rng, 6), axis_at), (parts,), jnp.float32, smallest / len(pieces), top_value / len(pieces))
        return jnp.repeat(jnp.exp(heights), shape[axis_at] // parts).reshape((-1,) + (1,) * (len(shape) - axis_at - 1))

    level = one(*pieces[0])
    for cut in pieces[1:]:
        level = level * one(*cut)
    return level


def deal_out(key, own, number, rows, number_of, top, bound, lean):
    ranking = jax.random.permutation(key, number_of)
    packed, ordinary = shares(number_of, rows * top, bound, lean, True), shares(number_of, rows * top, bound, lean, False)
    places = jnp.arange(number_of)

    def named(sizes, rotation):
        used = int((sizes > 0).sum())
        fixed = max(1, used // 4)
        moved = fixed + (places - fixed + rotation * (used - fixed)) % max(1, number_of - fixed)
        return jnp.zeros((number_of,), jnp.int32).at[ranking[jnp.where(places < fixed, places, moved)]].set(jnp.asarray(sizes, jnp.int32))

    sizes = jnp.where(number % 4 == 0, named(packed, number // 4), named(ordinary, number - number // 4 - 1))
    mixed = jax.random.permutation(jax.random.fold_in(own, 3), number_of)
    source_of, taker = mixed[0:number_of // 2 * 2:2], mixed[1:number_of // 2 * 2:2]
    slack = jnp.minimum(sizes[source_of] - 1, bound - sizes[taker]) // 2
    slack = jnp.where((source_of == ranking[0]) | (taker == ranking[0]) | (sizes[taker] == 0), 0, jnp.maximum(slack, 0))
    moved = jax.random.randint(jax.random.fold_in(own, 4), (number_of // 2,), 0, 1 << 20) % (slack + 1)
    sizes = sizes.at[source_of].add(-moved).at[taker].add(moved)
    items = jnp.searchsorted(jnp.cumsum(sizes), jnp.arange(rows * top), side="right").astype(jnp.int32)
    table = items.reshape(top, rows).T
    table = table[jax.random.permutation(jax.random.fold_in(own, 1), rows)]
    rotation = jax.random.randint(jax.random.fold_in(own, 2), (rows, 1), 0, top)
    return jnp.take_along_axis(table, (jnp.arange(top)[None, :] + rotation) % top, axis=1)


def shares(amount, total, limit, slope, full):
    loads = [(1 << 20) // math.isqrt(grade ** slope) + 1 for grade in range(1, amount + 1)]
    largest = limit if full else min(limit, max(-(-total // amount), total * loads[0] // sum(loads)))
    least = 1 if total - largest >= amount - 1 else 0
    given, surplus = [largest] + [least] * (amount - 1), total - largest - least * (amount - 1)
    while surplus > 0:
        free = [i for i in range(1, amount) if given[i] < largest] or [i for i in range(1, amount) if given[i] < limit]
        whole, left = sum([loads[i] for i in free]), surplus
        for i in free:
            more = min(limit - given[i], max(1, left * loads[i] // whole), surplus)
            given[i] = given[i] + more
            surplus = surplus - more
    return np.array(given)


def centred(own_key, extent, deviation, bound, cuts=(), kind=jnp.bfloat16):
    factor_of = block_scale(own_key, extent, cuts, -0.22, 0.18) if cuts else 1.0
    entries = jax.random.normal(own_key, extent, jnp.float32) * deviation * factor_of
    return jnp.minimum(jnp.maximum(entries, -bound), bound).astype(kind)


def setup_inputs(seed: int = 0) -> dict:
    key_list = jax.random.split(jax.random.key(seed), 10)
    tokens = centred(key_list[0], (TOKENS, D), 1.0, 6.0, ((0, 8), (1, 4)))
    routes_keys = jax.random.split(jax.random.fold_in(key_list[1], 1), TOKENS // TOK_DEV)
    routes_turns = jax.random.permutation(jax.random.fold_in(key_list[1], 3), TOKENS // TOK_DEV)
    routes = jax.vmap(lambda own, number: deal_out(jax.random.fold_in(key_list[1], 2), own, number, TOK_DEV, EXPERTS, TOP, CAP, 2))(routes_keys, routes_turns).reshape((TOKENS, TOP))
    route_weight = jnp.clip(jnp.exp(math.log(1.0) - 2.3025851 * jax.random.uniform(key_list[2], (TOKENS, TOP), jnp.float32) ** block_scale(key_list[2], (TOKENS, TOP), ((0, 8),), -0.2, 0.2)), 0.1, 1.0)
    gate_first = centred(key_list[3], (EXPERTS, BLOCKS, BW, RANK), BW ** -0.5, 0.5, ((0, 8), (1, 4)))
    up_first = centred(key_list[4], (EXPERTS, BLOCKS, BW, RANK), BW ** -0.5, 0.5, ((0, 8), (1, 4)))
    gate_second = centred(key_list[5], (EXPERTS, RANK, BLOCKS, BLOCKS), BLOCKS ** -0.5, 0.75, ((0, 8), (1, 4)))
    up_second = centred(key_list[6], (EXPERTS, RANK, BLOCKS, BLOCKS), BLOCKS ** -0.5, 0.75, ((0, 8), (1, 4)))
    down_first = centred(key_list[7], (EXPERTS, RANK, BLOCKS, BLOCKS), BLOCKS ** -0.5, 0.75, ((0, 8), (1, 4)))
    down_second = centred(key_list[8], (EXPERTS, BLOCKS, RANK, BW), RANK ** -0.5, 1.0, ((0, 8), (1, 4)))
    return dict(tokens=tokens, routes=routes, route_weight=route_weight, gate_first=gate_first, up_first=up_first, gate_second=gate_second, up_second=up_second, down_first=down_first, down_second=down_second)


def rounded(value):
    return lax.optimization_barrier(value.astype(jnp.bfloat16)).astype(jnp.float32)


def monarch_expert(picked_rows, expert_id, gate_first, up_first, gate_second, up_second, down_first, down_second):
    row_count = picked_rows.shape[0]
    shaped = picked_rows.reshape(row_count, BLOCKS, BW).astype(jnp.float32)
    gate_low = rounded(jnp.einsum("nbf,bfr->nbr", shaped, gate_first[expert_id].astype(jnp.float32)))
    up_low = rounded(jnp.einsum("nbf,bfr->nbr", shaped, up_first[expert_id].astype(jnp.float32)))
    gate_high = jnp.einsum("nbc,cbm->ncm", gate_low, gate_second[expert_id].astype(jnp.float32))
    up_high = jnp.einsum("nbc,cbm->ncm", up_low, up_second[expert_id].astype(jnp.float32))
    activated = rounded(jax.nn.silu(gate_high) * up_high)
    down_low = rounded(jnp.einsum("ncm,cmo->nco", activated, down_first[expert_id].astype(jnp.float32)))
    expert_out = jnp.einsum("ncb,bcf->nbf", down_low, down_second[expert_id].astype(jnp.float32))
    return expert_out.astype(jnp.bfloat16).reshape(row_count, D)


def reference(tokens, routes, route_weight, gate_first, up_first, gate_second, up_second, down_first, down_second):
    capacity_rows = N_EXPERT * CAP

    def one_expert(accumulated, expert_id):
        routed_here = routes == expert_id
        row_weight = jnp.sum(jnp.where(routed_here, route_weight, jnp.float32(0.0)), axis=1)
        chosen = jnp.any(routed_here, axis=1)
        picked_index = jnp.nonzero(chosen, size=capacity_rows, fill_value=TOKENS)[0].astype(jnp.int32)
        picked_rows = jnp.take(tokens, picked_index, axis=0, mode="fill", fill_value=0)
        expert_out = monarch_expert(picked_rows, expert_id, gate_first, up_first, gate_second, up_second, down_first, down_second)
        row_share = jnp.take(row_weight, picked_index, axis=0, mode="fill", fill_value=0)
        accumulated = accumulated.at[picked_index].add(expert_out.astype(jnp.float32) * row_share[:, None], mode="drop")
        return accumulated, jnp.sum(chosen.astype(jnp.int32))

    start = jnp.zeros((TOKENS, D), jnp.float32)
    accumulated, counts = lax.scan(one_expert, start, jnp.arange(EXPERTS, dtype=jnp.int32))
    moe_output = accumulated.astype(jnp.bfloat16)
    expert_load = counts.astype(jnp.float32) * EXPERTS / (TOKENS * TOP)
    return (moe_output, expert_load)
```

```python
import jax
import jax.numpy as jnp
from jax import lax
from jax.sharding import PartitionSpec as P


def shards(
    tokens,
    routes,
    route_weight,
    gate_first,
    up_first,
    gate_second,
    up_second,
    down_first,
    down_second,
):
    tok_rows, width_here = tokens.shape
    top_k = routes.shape[1]
    groups = lax.axis_size("expert")
    dp_count = lax.axis_size("dp")
    per_dev, blocks_here, block_width, rank_size = gate_first.shape
    rank_here = gate_second.shape[1]
    block_count = gate_second.shape[2]
    experts = per_dev * groups
    capacity = 2 * tok_rows * top_k // experts
    flat_routes = routes.reshape(-1)
    pair_count = flat_routes.shape[0]
    one_hot = (flat_routes[:, None] == jnp.arange(experts, dtype=jnp.int32)[None, :]).astype(
        jnp.int32
    )
    earlier = jnp.cumsum(one_hot, axis=0) - one_hot
    position = jnp.sum(earlier * one_hot, axis=1)
    counts = jnp.sum(one_hot, axis=0)
    slot_index = flat_routes * capacity + position
    pair_token = jnp.arange(pair_count, dtype=jnp.int32) // top_k
    slot_token = jnp.full((experts * capacity,), tok_rows, jnp.int32).at[slot_index].set(pair_token)
    outgoing = jnp.take(tokens, slot_token, axis=0, mode="fill", fill_value=0).reshape(
        groups, per_dev, capacity, width_here
    )
    gate_wide = gate_second.reshape(per_dev, rank_here, dp_count, blocks_here, block_count)
    up_wide = up_second.reshape(per_dev, rank_here, dp_count, blocks_here, block_count)
    down_wide = down_second.reshape(per_dev, blocks_here, dp_count, rank_here, block_width)
    received = lax.all_to_all(outgoing, "expert", split_axis=0, concat_axis=0, tiled=True)
    sources = received.shape[0]
    local = received.shape[1]
    slots = received.shape[2]
    split_rows = received.reshape(sources, local, slots, blocks_here, block_width)
    gate_low = jnp.einsum(
        "aesbf,ebfr->rbeas", split_rows, gate_first, preferred_element_type=jnp.float32
    )
    up_low = jnp.einsum(
        "aesbf,ebfr->rbeas", split_rows, up_first, preferred_element_type=jnp.float32
    )
    layout = (dp_count, rank_here, blocks_here, local, sources, slots)
    gate_mixed = lax.all_to_all(
        gate_low.astype(jnp.bfloat16).reshape(layout), "dp", split_axis=0, concat_axis=0, tiled=True
    )
    up_mixed = lax.all_to_all(
        up_low.astype(jnp.bfloat16).reshape(layout), "dp", split_axis=0, concat_axis=0, tiled=True
    )
    gate_high = jnp.einsum(
        "qcjeas,ecqjm->ecmas", gate_mixed, gate_wide, preferred_element_type=jnp.float32
    )
    up_high = jnp.einsum(
        "qcjeas,ecqjm->ecmas", up_mixed, up_wide, preferred_element_type=jnp.float32
    )
    activated = (jax.nn.silu(gate_high) * up_high).astype(jnp.bfloat16)
    down_low = jnp.einsum(
        "ecmas,ecmn->ecnas", activated, down_first, preferred_element_type=jnp.float32
    )
    down_split = down_low.astype(jnp.bfloat16).reshape(
        local, rank_here, dp_count, blocks_here, sources, slots
    )
    down_mixed = lax.all_to_all(down_split, "dp", split_axis=2, concat_axis=2, tiled=True)
    expert_out = jnp.einsum(
        "ecqjas,ejqcf->aesjf", down_mixed, down_wide, preferred_element_type=jnp.float32
    )
    result = expert_out.astype(jnp.bfloat16).reshape(sources, local, slots, width_here)
    totals = lax.psum(counts, "expert")
    own_counts = lax.dynamic_slice_in_dim(
        totals, lax.axis_index("expert") * per_dev, per_dev
    ).astype(jnp.float32)
    returned = lax.all_to_all(result, "expert", split_axis=0, concat_axis=0, tiled=True).reshape(
        experts * capacity, width_here
    )
    picked = jnp.take(returned, slot_index, axis=0).astype(jnp.float32)
    weighted = picked * route_weight.reshape(-1)[:, None]
    moe_output = jnp.sum(weighted.reshape(tok_rows, top_k, width_here), axis=1).astype(jnp.bfloat16)
    expert_load = own_counts * experts / (tok_rows * groups * top_k)
    return (moe_output, expert_load)


def spread_weights(dp_count, gate_first, up_first, gate_second, up_second, down_first, down_second):
    per_dev, blocks_here, block_width, rank_size = gate_first.shape
    rank_here, block_count = gate_second.shape[1:3]
    halves = 2
    half = blocks_here // halves
    same_block = jnp.eye(half, dtype=jnp.bfloat16)
    same_rank = jnp.eye(rank_here, dtype=jnp.bfloat16)
    same_side = jnp.eye(2, dtype=jnp.bfloat16)
    same_out = jnp.eye(blocks_here, dtype=jnp.bfloat16)
    first = jnp.stack([gate_first, up_first], axis=4).reshape(
        per_dev, halves, half, block_width, dp_count, rank_here, 2
    )
    first = jnp.einsum("ehjfqcg,jk->ehjfqgck", first, same_block).reshape(
        per_dev, halves, half * block_width, dp_count * 2 * rank_here * half
    )
    second = jnp.stack([gate_second, up_second], axis=1).reshape(
        per_dev, 2, rank_here, dp_count, halves, half, block_count
    )
    second = jnp.einsum("egcphjm,gk,cd->ephgcjkdm", second, same_side, same_rank).reshape(
        per_dev, 2 * rank_here * block_count, 2 * rank_here * block_count
    )
    third = down_first.reshape(per_dev, rank_here, block_count, dp_count, blocks_here)
    third = jnp.einsum("ecmpn,cd->ecmpdn", third, same_rank).reshape(
        per_dev, rank_here * block_count, rank_here * block_count
    )
    fourth = down_second.reshape(per_dev, blocks_here, dp_count, rank_here, block_width)
    fourth = jnp.einsum("enqcf,nk->eqcnkf", fourth, same_out).reshape(
        per_dev, rank_size * blocks_here, blocks_here * block_width
    )
    return first, second, third, fourth


def gathered(tokens, routes, route_weight, *weights):
    tok_rows, width_here = tokens.shape
    top_k = routes.shape[1]
    groups = lax.axis_size("expert")
    dp_count = lax.axis_size("dp")
    per_dev, blocks_here = weights[0].shape[:2]
    experts = per_dev * groups
    capacity = 2 * tok_rows * top_k // experts
    tokens_all = lax.all_gather(tokens, "expert")
    both = jnp.concatenate([routes.astype(jnp.float32), route_weight], axis=1)
    both = lax.all_gather(both, "expert")
    first, second, third, fourth = spread_weights(dp_count, *weights)
    halves = first.shape[1]
    mine = lax.axis_index("expert") * per_dev + jnp.arange(per_dev)
    named = both[:, :, :top_k, None] == mine.astype(jnp.float32)
    hit = jnp.any(named, axis=2)
    weight = jnp.sum(jnp.where(named, both[:, :, top_k:, None], 0.0), axis=2)
    ahead = jnp.tril(jnp.ones((tok_rows, tok_rows), jnp.bfloat16), -1)
    position = jnp.einsum(
        "tu,gue->gte", ahead, hit.astype(jnp.bfloat16), preferred_element_type=jnp.float32
    )
    position = jnp.where(hit, position, -1.0)
    slot = jnp.arange(capacity, dtype=jnp.float32)
    chosen = position[:, :, :, None] == slot
    dispatch = chosen.astype(jnp.bfloat16).reshape(groups, tok_rows, per_dev * capacity)
    combine = jnp.where(chosen, weight[:, :, :, None], 0.0).astype(jnp.bfloat16)
    combine = combine.reshape(groups, tok_rows, per_dev * capacity)
    rows = jnp.einsum(
        "gts,gtd->gsd", dispatch, tokens_all, preferred_element_type=jnp.float32
    ).astype(jnp.bfloat16)
    rows = rows.reshape(groups, per_dev, capacity, halves, width_here // halves)
    low = jnp.einsum(
        "geshk,ehkn->ehgsn", rows, first, preferred_element_type=jnp.float32
    ).astype(jnp.bfloat16)
    low = low.reshape(low.shape[:4] + (dp_count, -1))
    low = lax.all_to_all(low.transpose(4, 0, 1, 2, 3, 5), "dp", 0, 0, tiled=True)
    high = jnp.einsum(
        "pehgsk,ephkn->egsn",
        low,
        second.reshape(per_dev, dp_count, halves, -1, second.shape[2]),
        preferred_element_type=jnp.float32,
    )
    gate_high, up_high = jnp.split(high, 2, axis=-1)
    activated = (jax.nn.silu(gate_high) * up_high).astype(jnp.bfloat16)
    down = jnp.einsum(
        "egsk,ekn->egsn", activated, third, preferred_element_type=jnp.float32
    ).astype(jnp.bfloat16)
    down = down.reshape(down.shape[:3] + (dp_count, -1))
    down = lax.all_to_all(down.transpose(3, 0, 1, 2, 4), "dp", 0, 0, tiled=True)
    out = jnp.einsum(
        "qegsk,eqkd->gesd",
        down,
        fourth.reshape(per_dev, dp_count, -1, width_here),
        preferred_element_type=jnp.float32,
    ).astype(jnp.bfloat16)
    partial = jnp.einsum(
        "gts,gsd->gtd",
        combine,
        out.reshape(groups, per_dev * capacity, width_here),
        preferred_element_type=jnp.float32,
    ).astype(jnp.bfloat16)
    moe_output = lax.psum_scatter(partial, "expert", scatter_dimension=0)
    counts = jnp.sum(hit.astype(jnp.float32), axis=(0, 1))
    expert_load = counts * experts / (tok_rows * groups * top_k)
    return (moe_output, expert_load)


def chosen_plan(tokens, routes, *rest):
    groups = lax.axis_size("expert")
    if groups <= 2 * routes.shape[1]:
        return gathered(tokens, routes, *rest)
    return shards(tokens, routes, *rest)


def solution(mesh):
    return jax.shard_map(
        chosen_plan,
        mesh=mesh,
        in_specs=(
            P("expert", "dp"),
            P("expert", None),
            P("expert", None),
            P("expert", "dp", None, None),
            P("expert", "dp", None, None),
            P("expert", "dp", None, None),
            P("expert", "dp", None, None),
            P("expert", "dp", None, None),
            P("expert", "dp", None, None),
        ),
        out_specs=(P("expert", "dp"), P("expert")),
        check_vma=False,
    )
```

```python
import functools

import jax
import jax.numpy as jnp
from jax import lax
from jax.experimental import pallas as pl
from jax.experimental.pallas import tpu as pltpu
from jax.sharding import PartitionSpec as P

F32 = jnp.float32
BF16 = jnp.bfloat16
MESH = pl.DeviceIdType.MESH


def shards(
    tokens,
    routes,
    route_weight,
    gate_first,
    up_first,
    gate_second,
    up_second,
    down_first,
    down_second,
):
    tok_rows, width_here = tokens.shape
    top_k = routes.shape[1]
    groups = lax.axis_size("expert")
    dp_count = lax.axis_size("dp")
    per_dev, blocks_here, block_width, rank_size = gate_first.shape
    rank_here = gate_second.shape[1]
    block_count = gate_second.shape[2]
    experts = per_dev * groups
    capacity = 2 * tok_rows * top_k // experts
    flat_routes = routes.reshape(-1)
    pair_count = flat_routes.shape[0]
    one_hot = (flat_routes[:, None] == jnp.arange(experts, dtype=jnp.int32)[None, :]).astype(
        jnp.int32
    )
    earlier = jnp.cumsum(one_hot, axis=0) - one_hot
    position = jnp.sum(earlier * one_hot, axis=1)
    counts = jnp.sum(one_hot, axis=0)
    slot_index = flat_routes * capacity + position
    pair_token = jnp.arange(pair_count, dtype=jnp.int32) // top_k
    slot_token = jnp.full((experts * capacity,), tok_rows, jnp.int32).at[slot_index].set(pair_token)
    outgoing = jnp.take(tokens, slot_token, axis=0, mode="fill", fill_value=0).reshape(
        groups, per_dev, capacity, width_here
    )
    gate_wide = gate_second.reshape(per_dev, rank_here, dp_count, blocks_here, block_count)
    up_wide = up_second.reshape(per_dev, rank_here, dp_count, blocks_here, block_count)
    down_wide = down_second.reshape(per_dev, blocks_here, dp_count, rank_here, block_width)
    received = lax.all_to_all(outgoing, "expert", split_axis=0, concat_axis=0, tiled=True)
    sources = received.shape[0]
    local = received.shape[1]
    slots = received.shape[2]
    split_rows = received.reshape(sources, local, slots, blocks_here, block_width)
    gate_low = jnp.einsum(
        "aesbf,ebfr->rbeas", split_rows, gate_first, preferred_element_type=jnp.float32
    )
    up_low = jnp.einsum(
        "aesbf,ebfr->rbeas", split_rows, up_first, preferred_element_type=jnp.float32
    )
    layout = (dp_count, rank_here, blocks_here, local, sources, slots)
    gate_mixed = lax.all_to_all(
        gate_low.astype(jnp.bfloat16).reshape(layout), "dp", split_axis=0, concat_axis=0, tiled=True
    )
    up_mixed = lax.all_to_all(
        up_low.astype(jnp.bfloat16).reshape(layout), "dp", split_axis=0, concat_axis=0, tiled=True
    )
    gate_high = jnp.einsum(
        "qcjeas,ecqjm->ecmas", gate_mixed, gate_wide, preferred_element_type=jnp.float32
    )
    up_high = jnp.einsum(
        "qcjeas,ecqjm->ecmas", up_mixed, up_wide, preferred_element_type=jnp.float32
    )
    activated = (jax.nn.silu(gate_high) * up_high).astype(jnp.bfloat16)
    down_low = jnp.einsum(
        "ecmas,ecmn->ecnas", activated, down_first, preferred_element_type=jnp.float32
    )
    down_split = down_low.astype(jnp.bfloat16).reshape(
        local, rank_here, dp_count, blocks_here, sources, slots
    )
    down_mixed = lax.all_to_all(down_split, "dp", split_axis=2, concat_axis=2, tiled=True)
    expert_out = jnp.einsum(
        "ecqjas,ejqcf->aesjf", down_mixed, down_wide, preferred_element_type=jnp.float32
    )
    result = expert_out.astype(jnp.bfloat16).reshape(sources, local, slots, width_here)
    totals = lax.psum(counts, "expert")
    own_counts = lax.dynamic_slice_in_dim(
        totals, lax.axis_index("expert") * per_dev, per_dev
    ).astype(jnp.float32)
    returned = lax.all_to_all(result, "expert", split_axis=0, concat_axis=0, tiled=True).reshape(
        experts * capacity, width_here
    )
    picked = jnp.take(returned, slot_index, axis=0).astype(jnp.float32)
    weighted = picked * route_weight.reshape(-1)[:, None]
    moe_output = jnp.sum(weighted.reshape(tok_rows, top_k, width_here), axis=1).astype(jnp.bfloat16)
    expert_load = own_counts * experts / (tok_rows * groups * top_k)
    return (moe_output, expert_load)


def xor(a, b, count):
    total, bit = 0, 1
    while bit < count:
        total = total + bit * ((a // bit + b // bit) % 2)
        bit *= 2
    return total


def dot(a, b):
    return jnp.dot(a, b, preferred_element_type=F32)


def ones_at(shape, row_to_column):
    lead = shape[:-1]
    target = row_to_column(*[lax.broadcasted_iota(jnp.int32, shape, d) for d in range(len(lead))])
    column = lax.broadcasted_iota(jnp.int32, shape, len(lead))
    hit = jnp.where(column == target, F32(1), F32(0))
    return hit.reshape(-1, shape[-1]).astype(BF16)


def expert_kernel(
    sizes,
    tok, meta, gf, uf, gs, us, df, ds,
    out, counts,
    tok_all, meta_all, w1, w2, w3, w4, wide, rows, low_out, low_in, down_out, down_in,
    combine, made, own_part, x_out, x_in, z_out, z_in,
    tok_z, tok_x, tok_in, meta_z, meta_x, meta_in, low_s, low_r, down_s, down_r,
    local_s, x_s, x_r, z_s, z_r,
):
    groups, dp, top_k, cap = sizes
    per_dev, blocks, width, rank = gf.shape
    rank_here, block_count = gs.shape[1:3]
    tok_rows, features = tok.shape
    half = blocks // 2
    half_width = half * width
    chunk = 2 * rank_here * half
    pieces = 2 * dp
    hidden = rank_here * block_count
    slots = per_dev * cap
    nz = groups // 2
    d = lax.axis_index("dp")
    g = lax.axis_index("expert")
    z, x = g // 2, g % 2

    def at_dp(r):
        return (xor(d, r, dp), g)

    partner = (d, z * 2 + (1 - x))

    def at_z(k):
        return (d, xor(z, k, nz) * 2 + x)

    def remote(src, dst, send, recv, to):
        return pltpu.make_async_remote_copy(
            src_ref=src, dst_ref=dst, send_sem=send, recv_sem=recv,
            device_id=to, device_id_type=MESH,
        )

    barrier = pltpu.get_barrier_semaphore()
    peers = [at_dp(r) for r in range(1, dp)] + [partner] + [at_z(k) for k in range(1, nz)]
    for peer in peers:
        pl.semaphore_signal(barrier, inc=1, device_id=peer, device_id_type=MESH)
    pl.semaphore_wait(barrier, len(peers))

    def slot_of(k, b):
        return xor(z, k, nz) * 2 + (x + b) % 2

    def z_copies(k):
        return (
            remote(meta, meta_all.at[g], meta_z.at[k], meta_in.at[g], at_z(k)),
            remote(tok, tok_all.at[g], tok_z.at[k], tok_in.at[g], at_z(k)),
        )

    def x_copies(k):
        slot = slot_of(k, 0)
        return (
            remote(meta_all.at[slot], meta_all.at[slot], meta_x.at[k], meta_in.at[slot], partner),
            remote(tok_all.at[slot], tok_all.at[slot], tok_x.at[k], tok_in.at[slot], partner),
        )

    def own_x_copies():
        return (
            remote(meta, meta_all.at[g], meta_x.at[0], meta_in.at[g], partner),
            remote(tok, tok_all.at[g], tok_x.at[0], tok_in.at[g], partner),
        )

    def wait_slot(slot):
        remote(meta, meta_all.at[slot], meta_x.at[0], meta_in.at[slot], partner).wait_recv()
        remote(tok, tok_all.at[slot], tok_x.at[0], tok_in.at[slot], partner).wait_recv()

    for k in range(1, nz):
        for copy in z_copies(k):
            copy.start()
    for copy in own_x_copies():
        copy.start()
    tok_all[g] = tok[...]
    meta_all[g] = meta[...]
    counts[...] = jnp.zeros_like(counts)

    @pl.loop(0, blocks)
    def _(b):
        j = b % half
        places = [
            ones_at(
                (dp, rank_here, dp * chunk),
                lambda q, c: q * chunk + side * (chunk // 2) + c * half + j,
            )
            for side in range(2)
        ]
        value = dot(gf[:, b].reshape(-1, rank), places[0])
        value += dot(uf[:, b].reshape(-1, rank), places[1])
        w1[:, b] = value.astype(BF16).reshape(per_dev, width, dp * chunk)

    def spread_rest():
        wide[...] = jnp.zeros_like(wide)

        @pl.loop(0, per_dev)
        def _(e):
            for side, ref in enumerate((gs, us)):
                for c in range(rank_here):
                    lane = (c * block_count) % 128
                    value = dot(ref[e, c], ones_at((block_count, 128), lambda r: r + lane))
                    row = side * (chunk // 2) + c * half
                    start = side * hidden + c * block_count - lane
                    wide[:, row : row + half, start : start + 128] = value.reshape(
                        pieces, half, 128
                    )
            for piece in range(pieces):
                w2[e, piece] = wide[piece].astype(BF16)

        @pl.loop(0, rank_here)
        def _(c):
            place = ones_at((block_count, hidden), lambda r: r * rank_here + c)
            value = dot(df[:, c].reshape(-1, block_count), place)
            w3[:, c] = value.astype(BF16).reshape(per_dev, block_count, hidden)

        wide[...] = jnp.zeros_like(wide)

        @pl.loop(0, per_dev)
        def _(e):
            for n in range(blocks):
                h = n // half
                offset = (n % half) * width
                lane = offset % 128
                span = -(-(lane + width) // 128) * 128
                value = dot(ds[e, n], ones_at((width, span), lambda r: r + lane))
                wide[
                    h * dp : (h + 1) * dp,
                    n * rank_here : (n + 1) * rank_here,
                    offset - lane : offset - lane + span,
                ] = value.reshape(dp, rank_here, span)
            for q in range(dp):
                for h in range(2):
                    w4[e, q, :, h * half_width : (h + 1) * half_width] = wide[
                        h * dp + q, :, :half_width
                    ].astype(BF16)

    def place_of(i):
        last = groups - 1
        edge = 1 - (i % last + last - 1) // last
        return ((i + 1) // 2) % nz, (1 - i % 2 + edge) % 2

    def low_copy(i, r):
        return remote(
            low_out.at[i % 2, xor(d, r, dp)], low_in.at[i, d],
            low_s.at[i % 2, r], low_r.at[i, r], at_dp(r),
        )

    def down_copy(i, r):
        return remote(
            down_out.at[i % 2, xor(d, r, dp)], down_in.at[i, d],
            down_s.at[i % 2, r], down_r.at[i, r], at_dp(r),
        )

    def low_local(i):
        return pltpu.make_async_copy(low_out.at[i % 2, d], low_in.at[i, d], local_s.at[0])

    def down_local(i):
        return pltpu.make_async_copy(down_out.at[i % 2, d], down_in.at[i, d], local_s.at[1])

    crossing = list(range(dp - 1, 0, -1))

    def stage_a(i):
        k, b = place_of(i)
        slot = slot_of(k, b)

        @pl.when(b == 1)
        def _():
            wait_slot(slot)

        @pl.when(i >= 2)
        def _():
            for r in crossing:
                low_copy(i, r).wait_send()

        info = meta_all[slot]
        named_rows, weights = info[:top_k], info[top_k:]
        line = lax.broadcasted_iota(jnp.int32, (8, tok_rows), 0)
        hits = jnp.zeros((8, tok_rows), F32)
        shares = []
        for e in range(per_dev):
            named = named_rows == (g * per_dev + e).astype(F32)
            hit = jnp.max(jnp.where(named, F32(1), F32(0)), axis=0, keepdims=True)
            hits = hits + jnp.where(line == e, hit, F32(0))
            shares.append(jnp.sum(jnp.where(named, weights, F32(0)), axis=0, keepdims=True))
        counts[...] += hits
        before = lax.broadcasted_iota(jnp.int32, (tok_rows, tok_rows), 0)
        after = lax.broadcasted_iota(jnp.int32, (tok_rows, tok_rows), 1)
        ahead = jnp.where(before < after, F32(1), F32(0)).astype(BF16)
        position = dot(hits.astype(BF16), ahead)
        position = jnp.where(hits > 0, position, F32(-1)).astype(jnp.int32)
        slot_row = lax.broadcasted_iota(jnp.int32, (cap, tok_rows), 0)
        pick, mix = [], []
        for e in range(per_dev):
            chosen = slot_row == position[e : e + 1]
            pick.append(jnp.where(chosen, F32(1), F32(0)))
            mix.append(jnp.where(chosen, shares[e], F32(0)))
        pick = jnp.concatenate(pick, axis=0).astype(BF16)
        combine[i] = jnp.concatenate(mix, axis=0).T.astype(BF16)
        rows[...] = dot(pick, tok_all[slot]).astype(BF16)
        for e in range(per_dev):
            span = slice(e * cap, (e + 1) * cap)
            for h in range(2):
                weight = w1[e, h * half : (h + 1) * half].reshape(half_width, dp * chunk)
                low = dot(rows[span, h * half_width : (h + 1) * half_width], weight).astype(BF16)
                for q in range(dp):
                    low_out[i % 2, q, h, span, :] = low[:, q * chunk : (q + 1) * chunk]
        for r in crossing:
            low_copy(i, r).start()
        low_local(i).start()
        low_local(i).wait()

        @pl.when((i % 2 == 0) & (i // 2 + 1 < nz))
        def _():
            after = i // 2 + 1
            wait_slot(slot_of(after, 0))
            for copy in x_copies(after):
                copy.start()

    def stage_b(i):
        for r in crossing:
            low_copy(i, r).wait_recv()

        @pl.when(i >= 2)
        def _():
            for r in crossing:
                down_copy(i, r).wait_send()

        for e in range(per_dev):
            span = slice(e * cap, (e + 1) * cap)
            low = jnp.concatenate(
                [low_in[i, p, h, span, :] for p in range(dp) for h in range(2)], axis=1
            )
            high = dot(low, w2[e].reshape(pieces * chunk, 2 * hidden))
            gate, up = high[:, :hidden], high[:, hidden:]
            activated = (gate / (1 + jnp.exp(-gate)) * up).astype(BF16)
            down = dot(activated, w3[e].reshape(hidden, hidden)).astype(BF16)
            for p in range(dp):
                down_out[i % 2, p, span, :] = down[:, p * chunk : (p + 1) * chunk]
        for r in crossing:
            down_copy(i, r).start()
        down_local(i).start()
        down_local(i).wait()

    def x_part(k):
        return remote(x_out.at[k], x_in.at[k], x_s.at[k], x_r.at[k], partner)

    def z_part(k):
        return remote(z_out.at[k], z_in.at[k], z_s.at[k], z_r.at[k], at_z(k))

    def stage_c(i):
        k, b = place_of(i)
        for r in crossing:
            down_copy(i, r).wait_recv()
        for e in range(per_dev):
            span = slice(e * cap, (e + 1) * cap)
            down = jnp.concatenate([down_in[i, q, span, :] for q in range(dp)], axis=1)
            made[span, :] = dot(down, w4[e].reshape(dp * chunk, features)).astype(BF16)
        part = dot(combine[i], made[...]).astype(BF16)

        @pl.when(b == 0)
        def _():
            own_part[k] = part

        @pl.when(b == 1)
        def _():
            x_out[k] = part
            x_part(k).start()

    def pass_on(k):
        x_part(k).wait_recv()
        z_out[k] = (own_part[k].astype(F32) + x_in[k].astype(F32)).astype(BF16)
        z_part(k).start()

    @pl.loop(0, groups + 2)
    def _(step):
        @pl.when(step < groups)
        def _():
            stage_a(step)

        @pl.when(step == 0)
        def _():
            spread_rest()

        @pl.when((step >= 1) & (step <= groups))
        def _():
            stage_b(step - 1)

        @pl.when((step >= 5) & (step % 2 == 1))
        def _():
            pass_on((step - 3) // 2)

        @pl.when(step >= 2)
        def _():
            stage_c(step - 2)

    x_part(0).wait_recv()
    total = own_part[0].astype(F32) + x_in[0].astype(F32)
    for k in range(1, nz):
        z_part(k).wait_recv()
        total += z_in[k].astype(F32)
    out[...] = total.astype(BF16)

    for k in range(1, nz):
        for copy in z_copies(k):
            copy.wait_send()
        for copy in x_copies(k):
            copy.wait_send()
        z_part(k).wait_send()
    for copy in own_x_copies():
        copy.wait_send()
    for k in range(nz):
        x_part(k).wait_send()
    for i in (groups - 2, groups - 1):
        for r in crossing:
            low_copy(i, r).wait_send()
            down_copy(i, r).wait_send()


def fused(tokens, routes, route_weight, *weights):
    tok_rows, features = tokens.shape
    top_k = routes.shape[1]
    groups = lax.axis_size("expert")
    dp = lax.axis_size("dp")
    per_dev, blocks, width, rank = weights[0].shape
    rank_here, block_count = weights[2].shape[1:3]
    experts = per_dev * groups
    cap = 2 * tok_rows * top_k // experts
    nz = groups // 2
    chunk = 2 * rank_here * (blocks // 2)
    hidden = rank_here * block_count
    slots = per_dev * cap
    meta = jnp.concatenate([routes.T.astype(F32), route_weight.T], axis=0)
    vmem = pl.BlockSpec(memory_space=pltpu.VMEM)
    dma = pltpu.SemaphoreType.DMA
    out, counts = pl.pallas_call(
        functools.partial(expert_kernel, (groups, dp, top_k, cap)),
        out_shape=(
            jax.ShapeDtypeStruct((tok_rows, features), BF16),
            jax.ShapeDtypeStruct((8, tok_rows), F32),
        ),
        in_specs=[vmem] * 8,
        out_specs=(vmem, vmem),
        scratch_shapes=[
            pltpu.VMEM((groups, tok_rows, features), BF16),
            pltpu.VMEM((groups, 2 * top_k, tok_rows), F32),
            pltpu.VMEM((per_dev, blocks, width, dp * chunk), BF16),
            pltpu.VMEM((per_dev, 2 * dp, chunk, 2 * hidden), BF16),
            pltpu.VMEM((per_dev, rank_here, block_count, hidden), BF16),
            pltpu.VMEM((per_dev, dp, chunk, features), BF16),
            pltpu.VMEM((2 * dp, chunk, 2 * hidden), F32),
            pltpu.VMEM((slots, features), BF16),
            pltpu.VMEM((2, dp, 2, slots, chunk), BF16),
            pltpu.VMEM((groups, dp, 2, slots, chunk), BF16),
            pltpu.VMEM((2, dp, slots, chunk), BF16),
            pltpu.VMEM((groups, dp, slots, chunk), BF16),
            pltpu.VMEM((groups, tok_rows, slots), BF16),
            pltpu.VMEM((slots, features), BF16),
            pltpu.VMEM((nz, tok_rows, features), BF16),
            pltpu.VMEM((nz, tok_rows, features), BF16),
            pltpu.VMEM((nz, tok_rows, features), BF16),
            pltpu.VMEM((nz, tok_rows, features), BF16),
            pltpu.VMEM((nz, tok_rows, features), BF16),
            dma((nz,)), dma((nz,)), dma((groups,)),
            dma((nz,)), dma((nz,)), dma((groups,)),
            dma((2, dp)), dma((groups, dp)), dma((2, dp)), dma((groups, dp)),
            dma((2,)), dma((nz,)), dma((nz,)), dma((nz,)), dma((nz,)),
        ],
        compiler_params=pltpu.CompilerParams(
            collective_id=0, has_side_effects=True, vmem_limit_bytes=67043328
        ),
    )(tokens, meta, *weights)
    held = jnp.sum(counts, axis=1)[:per_dev]
    return (out, held * experts / (tok_rows * groups * top_k))


def chosen_plan(tokens, routes, route_weight, *weights):
    groups = lax.axis_size("expert")
    dp = lax.axis_size("dp")
    blocks, width = weights[0].shape[1:3]
    rank_here, block_count = weights[2].shape[1:3]
    tiled = (
        tokens.shape[0] % 128 == 0
        and 2 * rank_here * (blocks // 2) == 128
        and rank_here == 8
        and weights[0].shape[0] <= 8
        and blocks // 2 == 8
        and block_count == 2 * dp * 8
        and (blocks // 2 * width) % 128 == 0
    )
    powers = groups & (groups - 1) == 0 and dp & (dp - 1) == 0
    if groups <= 2 * routes.shape[1] and groups >= 4 and dp >= 2 and powers and tiled:
        return fused(tokens, routes, route_weight, *weights)
    return shards(tokens, routes, route_weight, *weights)


def solution(mesh):
    return jax.shard_map(
        chosen_plan,
        mesh=mesh,
        in_specs=(
            P("expert", "dp"),
            P("expert", None),
            P("expert", None),
            P("expert", "dp", None, None),
            P("expert", "dp", None, None),
            P("expert", "dp", None, None),
            P("expert", "dp", None, None),
            P("expert", "dp", None, None),
            P("expert", "dp", None, None),
        ),
        out_specs=(P("expert", "dp"), P("expert")),
        check_vma=False,
    )
```

```python
import functools

import jax
import jax.numpy as jnp
from jax import lax
from jax.experimental import pallas as pl
from jax.experimental.pallas import tpu as pltpu
from jax.sharding import PartitionSpec as P

F32 = jnp.float32
BF16 = jnp.bfloat16
MESH = pl.DeviceIdType.MESH


def shards(
    tokens,
    routes,
    route_weight,
    gate_first,
    up_first,
    gate_second,
    up_second,
    down_first,
    down_second,
):
    tok_rows, width_here = tokens.shape
    top_k = routes.shape[1]
    groups = lax.axis_size("expert")
    dp_count = lax.axis_size("dp")
    per_dev, blocks_here, block_width, rank_size = gate_first.shape
    rank_here = gate_second.shape[1]
    block_count = gate_second.shape[2]
    experts = per_dev * groups
    capacity = 2 * tok_rows * top_k // experts
    flat_routes = routes.reshape(-1)
    pair_count = flat_routes.shape[0]
    one_hot = (flat_routes[:, None] == jnp.arange(experts, dtype=jnp.int32)[None, :]).astype(
        jnp.int32
    )
    earlier = jnp.cumsum(one_hot, axis=0) - one_hot
    position = jnp.sum(earlier * one_hot, axis=1)
    counts = jnp.sum(one_hot, axis=0)
    slot_index = flat_routes * capacity + position
    pair_token = jnp.arange(pair_count, dtype=jnp.int32) // top_k
    slot_token = jnp.full((experts * capacity,), tok_rows, jnp.int32).at[slot_index].set(pair_token)
    outgoing = jnp.take(tokens, slot_token, axis=0, mode="fill", fill_value=0).reshape(
        groups, per_dev, capacity, width_here
    )
    gate_wide = gate_second.reshape(per_dev, rank_here, dp_count, blocks_here, block_count)
    up_wide = up_second.reshape(per_dev, rank_here, dp_count, blocks_here, block_count)
    down_wide = down_second.reshape(per_dev, blocks_here, dp_count, rank_here, block_width)
    received = lax.all_to_all(outgoing, "expert", split_axis=0, concat_axis=0, tiled=True)
    sources = received.shape[0]
    local = received.shape[1]
    slots = received.shape[2]
    split_rows = received.reshape(sources, local, slots, blocks_here, block_width)
    gate_low = jnp.einsum(
        "aesbf,ebfr->rbeas", split_rows, gate_first, preferred_element_type=jnp.float32
    )
    up_low = jnp.einsum(
        "aesbf,ebfr->rbeas", split_rows, up_first, preferred_element_type=jnp.float32
    )
    layout = (dp_count, rank_here, blocks_here, local, sources, slots)
    gate_mixed = lax.all_to_all(
        gate_low.astype(jnp.bfloat16).reshape(layout), "dp", split_axis=0, concat_axis=0, tiled=True
    )
    up_mixed = lax.all_to_all(
        up_low.astype(jnp.bfloat16).reshape(layout), "dp", split_axis=0, concat_axis=0, tiled=True
    )
    gate_high = jnp.einsum(
        "qcjeas,ecqjm->ecmas", gate_mixed, gate_wide, preferred_element_type=jnp.float32
    )
    up_high = jnp.einsum(
        "qcjeas,ecqjm->ecmas", up_mixed, up_wide, preferred_element_type=jnp.float32
    )
    activated = (jax.nn.silu(gate_high) * up_high).astype(jnp.bfloat16)
    down_low = jnp.einsum(
        "ecmas,ecmn->ecnas", activated, down_first, preferred_element_type=jnp.float32
    )
    down_split = down_low.astype(jnp.bfloat16).reshape(
        local, rank_here, dp_count, blocks_here, sources, slots
    )
    down_mixed = lax.all_to_all(down_split, "dp", split_axis=2, concat_axis=2, tiled=True)
    expert_out = jnp.einsum(
        "ecqjas,ejqcf->aesjf", down_mixed, down_wide, preferred_element_type=jnp.float32
    )
    result = expert_out.astype(jnp.bfloat16).reshape(sources, local, slots, width_here)
    totals = lax.psum(counts, "expert")
    own_counts = lax.dynamic_slice_in_dim(
        totals, lax.axis_index("expert") * per_dev, per_dev
    ).astype(jnp.float32)
    returned = lax.all_to_all(result, "expert", split_axis=0, concat_axis=0, tiled=True).reshape(
        experts * capacity, width_here
    )
    picked = jnp.take(returned, slot_index, axis=0).astype(jnp.float32)
    weighted = picked * route_weight.reshape(-1)[:, None]
    moe_output = jnp.sum(weighted.reshape(tok_rows, top_k, width_here), axis=1).astype(jnp.bfloat16)
    expert_load = own_counts * experts / (tok_rows * groups * top_k)
    return (moe_output, expert_load)


def xor(a, b, count):
    total, bit = 0, 1
    while bit < count:
        total = total + bit * ((a // bit + b // bit) % 2)
        bit *= 2
    return total


def dot(a, b):
    return jnp.dot(a, b, preferred_element_type=F32)


def ones_at(shape, row_to_column):
    lead = shape[:-1]
    target = row_to_column(*[lax.broadcasted_iota(jnp.int32, shape, d) for d in range(len(lead))])
    column = lax.broadcasted_iota(jnp.int32, shape, len(lead))
    hit = jnp.where(column == target, F32(1), F32(0))
    return hit.reshape(-1, shape[-1]).astype(BF16)


def expert_kernel(
    sizes,
    tok, routes, shares_in, gf, uf, gs, df, ds,
    out, load,
    tok_all, routes_all, shares_all, gf2, uf2, gs2, df2, ds2,
    w1, w2, w3, w4, wide, rows, low_out, low_in, down_out, down_in,
    combine, made, summed, z_out, z_in, counts, counts_in,
    gather_s, gather_r, weight_s, weight_r, low_s, low_r, down_s, down_r,
    local_s, count_s, z_s, z_r,
):
    groups, dp, top_k, cap, rank_here, block_count = sizes
    per_dev, blocks, rank, width = gf.shape
    tok_rows, features = tok.shape
    experts = per_dev * groups
    half = blocks // 2
    half_width = half * width
    chunk = 2 * rank_here * half
    pieces = 2 * dp
    hidden = rank_here * block_count
    nz = groups // 2
    total_steps = 2 * nz
    d = lax.axis_index("dp")
    g = lax.axis_index("expert")
    z, x = g // 2, g % 2
    partner = (d, z * 2 + (1 - x))

    def at_dp(r):
        return (xor(d, r, dp), g)

    def at_z(k):
        return (d, xor(z, k, nz) * 2 + x)

    def remote(src, dst, send, recv, to):
        return pltpu.make_async_remote_copy(
            src_ref=src, dst_ref=dst, send_sem=send, recv_sem=recv,
            device_id=to, device_id_type=MESH,
        )

    barrier = pltpu.get_barrier_semaphore()
    peers = [at_dp(r) for r in range(1, dp)] + [partner] + [at_z(k) for k in range(1, nz)]
    for peer in peers:
        pl.semaphore_signal(barrier, inc=1, device_id=peer, device_id_type=MESH)
    pl.semaphore_wait(barrier, len(peers))

    def gather(k):
        pairs = ((routes, routes_all), (shares_in, shares_all), (tok, tok_all))
        return [
            remote(src, dst.at[k], gather_s.at[n, k], gather_r.at[n, k], at_z(k))
            for n, (src, dst) in enumerate(pairs)
        ]

    held = (gf, uf, gs, df, ds)
    swapped = (gf2, uf2, gs2, df2, ds2)

    def swap(n):
        return remote(held[n], swapped[n], weight_s.at[n], weight_r.at[n], partner)

    for k in range(1, nz):
        for copy in gather(k):
            copy.start()
    for n in range(len(held)):
        swap(n).start()
    tok_all[0] = tok[...]
    routes_all[0] = routes[...]
    shares_all[0] = shares_in[...]
    counts[...] = jnp.zeros_like(counts)

    def spread_first(gate, up):
        @pl.loop(0, blocks)
        def _(b):
            j = b % half
            place = ones_at(
                (2, dp, rank_here, dp * chunk),
                lambda side, q, c: q * chunk + side * (chunk // 2) + c * half + j,
            )
            for e in range(per_dev):
                both = jnp.concatenate([gate[e, b], up[e, b]], axis=0)
                w1[e, b] = lax.dot_general(
                    both, place, (((0,), (0,)), ((), ())), preferred_element_type=F32
                ).astype(BF16)

    def spread_middle(second, third):
        wide[...] = jnp.zeros_like(wide)

        @pl.loop(0, per_dev)
        def _(e):
            for side in range(2):
                for c in range(rank_here):
                    lane = (c * block_count) % 128
                    place = ones_at(
                        (2, block_count, 128),
                        lambda s, r: jnp.where(s == side, r + lane, -1),
                    )
                    value = dot(second[e, c], place)
                    row = side * (chunk // 2) + c * half
                    start = side * hidden + c * block_count - lane
                    wide[:, row : row + half, start : start + 128] = value.reshape(
                        pieces, half, 128
                    )
            for piece in range(pieces):
                w2[e, piece] = wide[piece].astype(BF16)

        @pl.loop(0, rank_here)
        def _(c):
            pairs = rank_here // 2
            place = ones_at(
                (2, block_count, hidden),
                lambda s, r: jnp.where(s == c // pairs, r * rank_here + c, -1),
            )
            value = dot(third[:, c % pairs].reshape(-1, 2 * block_count), place)
            w3[:, c] = value.astype(BF16).reshape(per_dev, block_count, hidden)

    def spread_last(fourth):
        wide[...] = jnp.zeros_like(wide)

        @pl.loop(0, per_dev)
        def _(e):
            for n in range(blocks):
                h = n // half
                offset = (n % half) * width
                lane = offset % 128
                span = -(-(lane + width) // 128) * 128
                value = dot(fourth[e, n], ones_at((width, span), lambda r: r + lane))
                wide[
                    h * dp : (h + 1) * dp,
                    n * rank_here : (n + 1) * rank_here,
                    offset - lane : offset - lane + span,
                ] = value.reshape(dp, rank_here, span)
            for q in range(dp):
                for h in range(2):
                    w4[e, q, :, h * half_width : (h + 1) * half_width] = wide[
                        h * dp + q, :, :half_width
                    ].astype(BF16)

    def place_of(i):
        turn = i // nz
        return turn, (i % nz) * (1 - turn) + (nz - 1 - i % nz) * turn

    def low_copy(i, r):
        return remote(
            low_out.at[i % 2, xor(d, r, dp)], low_in.at[i, d],
            low_s.at[i % 2, r], low_r.at[i, r], at_dp(r),
        )

    def down_copy(i, r):
        return remote(
            down_out.at[i % 2, xor(d, r, dp)], down_in.at[i, d],
            down_s.at[i % 2, r], down_r.at[i, r], at_dp(r),
        )

    def low_local(i):
        return pltpu.make_async_copy(low_out.at[i % 2, d], low_in.at[i, d], local_s.at[0])

    def down_local(i):
        return pltpu.make_async_copy(down_out.at[i % 2, d], down_in.at[i, d], local_s.at[1])

    crossing = list(range(dp - 1, 0, -1))

    def stage_a(i):
        turn, k = place_of(i)

        @pl.when((turn == 0) & (k > 0))
        def _():
            for copy in gather(k):
                copy.wait_recv()

        @pl.when(i >= 2)
        def _():
            for r in crossing:
                low_copy(i, r).wait_send()

        base = (z * 2 + (x + turn) % 2) * per_dev
        named_rows, weights = routes_all[k], shares_all[k]
        line = lax.broadcasted_iota(jnp.int32, (8, tok_rows), 0)
        hits = jnp.zeros((8, tok_rows), F32)
        shares = []
        for e in range(per_dev):
            named = named_rows == base + e
            hit = jnp.max(jnp.where(named, F32(1), F32(0)), axis=0, keepdims=True)
            hits = hits + jnp.where(line == e, hit, F32(0))
            shares.append(jnp.sum(jnp.where(named, weights, F32(0)), axis=0, keepdims=True))
        counts[turn] += hits
        before = lax.broadcasted_iota(jnp.int32, (tok_rows, tok_rows), 0)
        after = lax.broadcasted_iota(jnp.int32, (tok_rows, tok_rows), 1)
        ahead = jnp.where(before < after, F32(1), F32(0)).astype(BF16)
        position = dot(hits.astype(BF16), ahead)
        position = jnp.where(hits > 0, position, F32(-1)).astype(jnp.int32)
        slot_row = lax.broadcasted_iota(jnp.int32, (cap, tok_rows), 0)
        pick, mix = [], []
        for e in range(per_dev):
            chosen = slot_row == position[e : e + 1]
            pick.append(jnp.where(chosen, F32(1), F32(0)))
            mix.append(jnp.where(chosen, shares[e], F32(0)))
        pick = jnp.concatenate(pick, axis=0).astype(BF16)
        combine[i] = jnp.concatenate(mix, axis=0).T.astype(BF16)
        rows[...] = dot(pick, tok_all[k]).astype(BF16)
        for e in range(per_dev):
            span = slice(e * cap, (e + 1) * cap)
            for h in range(2):
                weight = w1[e, h * half : (h + 1) * half].reshape(half_width, dp * chunk)
                low = dot(rows[span, h * half_width : (h + 1) * half_width], weight).astype(BF16)
                for q in range(dp):
                    low_out[i % 2, q, h, span, :] = low[:, q * chunk : (q + 1) * chunk]
        for r in crossing:
            low_copy(i, r).start()
        low_local(i).start()
        low_local(i).wait()

    def stage_b(i):
        for r in crossing:
            low_copy(i, r).wait_recv()

        @pl.when(i >= 2)
        def _():
            for r in crossing:
                down_copy(i, r).wait_send()

        for e in range(per_dev):
            span = slice(e * cap, (e + 1) * cap)
            low = jnp.concatenate(
                [low_in[i, p, h, span, :] for p in range(dp) for h in range(2)], axis=1
            )
            high = dot(low, w2[e].reshape(pieces * chunk, 2 * hidden))
            gate, up = high[:, :hidden], high[:, hidden:]
            activated = (gate / (1 + jnp.exp(-gate)) * up).astype(BF16)
            down = dot(activated, w3[e].reshape(hidden, hidden)).astype(BF16)
            for p in range(dp):
                down_out[i % 2, p, span, :] = down[:, p * chunk : (p + 1) * chunk]
        for r in crossing:
            down_copy(i, r).start()
        down_local(i).start()
        down_local(i).wait()

    def z_part(k):
        return remote(z_out.at[k], z_in.at[k], z_s.at[k], z_r.at[k], at_z(k))

    def stage_c(i):
        turn, k = place_of(i)
        for r in crossing:
            down_copy(i, r).wait_recv()
        for e in range(per_dev):
            span = slice(e * cap, (e + 1) * cap)
            down = jnp.concatenate([down_in[i, q, span, :] for q in range(dp)], axis=1)
            made[span, :] = dot(down, w4[e].reshape(dp * chunk, features)).astype(BF16)
        part = dot(combine[i], made[...])

        @pl.when(turn == 0)
        def _():
            summed[k] = part

        @pl.when((turn == 1) & (k == 0))
        def _():
            summed[k] += part

        @pl.when((turn == 1) & (k > 0))
        def _():
            z_out[k] = (summed[k] + part).astype(BF16)
            z_part(k).start()

    count_copy = remote(counts.at[1], counts_in, count_s.at[0], count_s.at[1], partner)

    spread_first(gf, uf)

    @pl.loop(0, total_steps + 2)
    def _(step):
        @pl.when(step == nz)
        def _():
            swap(0).wait_recv()
            swap(1).wait_recv()
            spread_first(gf2, uf2)

        @pl.when(step < total_steps)
        def _():
            stage_a(step)

        @pl.when(step == 0)
        def _():
            spread_middle(gs, df)
            spread_last(ds)

        @pl.when(step == total_steps)
        def _():
            count_copy.start()

        @pl.when(step == nz + 1)
        def _():
            swap(2).wait_recv()
            swap(3).wait_recv()
            spread_middle(gs2, df2)

        @pl.when((step >= 1) & (step <= total_steps))
        def _():
            stage_b(step - 1)

        @pl.when(step == nz + 2)
        def _():
            swap(4).wait_recv()
            spread_last(ds2)

        @pl.when(step >= 2)
        def _():
            stage_c(step - 2)

    count_copy.wait()
    ones = jnp.ones((8, tok_rows), BF16)
    held_rows = lax.dot_general(
        ones, (counts[0] + counts_in[...]).astype(BF16),
        (((1,), (1,)), ((), ())), preferred_element_type=F32,
    )
    load[...] = held_rows[:1, :per_dev] * experts / (tok_rows * groups * top_k)

    total = summed[0]
    for k in range(1, nz):
        z_part(k).wait_recv()
        total += z_in[k].astype(F32)
    out[...] = total.astype(BF16)

    for k in range(1, nz):
        for copy in gather(k):
            copy.wait_send()
        z_part(k).wait_send()
    for n in range(len(held)):
        swap(n).wait_send()
    for i in (total_steps - 2, total_steps - 1):
        for r in crossing:
            low_copy(i, r).wait_send()
            down_copy(i, r).wait_send()


def fused(
    tokens, routes, route_weight,
    gate_first, up_first, gate_second, up_second, down_first, down_second,
):
    tok_rows, features = tokens.shape
    top_k = routes.shape[1]
    groups = lax.axis_size("expert")
    dp = lax.axis_size("dp")
    per_dev, blocks, width, rank = gate_first.shape
    rank_here, block_count = gate_second.shape[1:3]
    experts = per_dev * groups
    cap = 2 * tok_rows * top_k // experts
    nz = groups // 2
    steps = 2 * nz
    chunk = 2 * rank_here * (blocks // 2)
    hidden = rank_here * block_count
    slots = per_dev * cap
    pairs = rank_here // 2
    factors = (
        gate_first.swapaxes(2, 3),
        up_first.swapaxes(2, 3),
        jnp.concatenate([gate_second, up_second], axis=3),
        jnp.concatenate([down_first[:, :pairs], down_first[:, pairs:]], axis=3),
        down_second,
    )
    vmem = pl.BlockSpec(memory_space=pltpu.VMEM)
    dma = pltpu.SemaphoreType.DMA
    out, load = pl.pallas_call(
        functools.partial(expert_kernel, (groups, dp, top_k, cap, rank_here, block_count)),
        out_shape=(
            jax.ShapeDtypeStruct((tok_rows, features), BF16),
            jax.ShapeDtypeStruct((1, per_dev), F32),
        ),
        in_specs=[vmem] * 8,
        out_specs=(vmem, vmem),
        scratch_shapes=[
            pltpu.VMEM((nz, tok_rows, features), BF16),
            pltpu.VMEM((nz, top_k, tok_rows), jnp.int32),
            pltpu.VMEM((nz, top_k, tok_rows), F32),
            *[pltpu.VMEM(factor.shape, BF16) for factor in factors],
            pltpu.VMEM((per_dev, blocks, width, dp * chunk), BF16),
            pltpu.VMEM((per_dev, 2 * dp, chunk, 2 * hidden), BF16),
            pltpu.VMEM((per_dev, rank_here, block_count, hidden), BF16),
            pltpu.VMEM((per_dev, dp, chunk, features), BF16),
            pltpu.VMEM((2 * dp, chunk, 2 * hidden), F32),
            pltpu.VMEM((slots, features), BF16),
            pltpu.VMEM((2, dp, 2, slots, chunk), BF16),
            pltpu.VMEM((steps, dp, 2, slots, chunk), BF16),
            pltpu.VMEM((2, dp, slots, chunk), BF16),
            pltpu.VMEM((steps, dp, slots, chunk), BF16),
            pltpu.VMEM((steps, tok_rows, slots), BF16),
            pltpu.VMEM((slots, features), BF16),
            pltpu.VMEM((nz, tok_rows, features), F32),
            pltpu.VMEM((nz, tok_rows, features), BF16),
            pltpu.VMEM((nz, tok_rows, features), BF16),
            pltpu.VMEM((2, 8, tok_rows), F32),
            pltpu.VMEM((8, tok_rows), F32),
            dma((3, nz)), dma((3, nz)), dma((5,)), dma((5,)),
            dma((2, dp)), dma((steps, dp)), dma((2, dp)), dma((steps, dp)),
            dma((2,)), dma((2,)), dma((nz,)), dma((nz,)),
        ],
        compiler_params=pltpu.CompilerParams(
            collective_id=0, has_side_effects=True, vmem_limit_bytes=67043328
        ),
    )(tokens, routes.T, route_weight.T, *factors)
    return (out, load.reshape(per_dev))


def chosen_plan(tokens, routes, route_weight, *weights):
    groups = lax.axis_size("expert")
    dp = lax.axis_size("dp")
    blocks, width = weights[0].shape[1:3]
    rank_here, block_count = weights[2].shape[1:3]
    tiled = (
        tokens.shape[0] % 128 == 0
        and 2 * rank_here * (blocks // 2) == 128
        and rank_here == 8
        and weights[0].shape[0] <= 8
        and blocks // 2 == 8
        and block_count == 2 * dp * 8
        and (blocks // 2 * width) % 128 == 0
    )
    powers = groups & (groups - 1) == 0 and dp & (dp - 1) == 0
    if groups <= 2 * routes.shape[1] and groups >= 4 and dp >= 2 and powers and tiled:
        return fused(tokens, routes, route_weight, *weights)
    return shards(tokens, routes, route_weight, *weights)


def solution(mesh):
    return jax.shard_map(
        chosen_plan,
        mesh=mesh,
        in_specs=(
            P("expert", "dp"),
            P("expert", None),
            P("expert", None),
            P("expert", "dp", None, None),
            P("expert", "dp", None, None),
            P("expert", "dp", None, None),
            P("expert", "dp", None, None),
            P("expert", "dp", None, None),
            P("expert", "dp", None, None),
        ),
        out_specs=(P("expert", "dp"), P("expert")),
        check_vma=False,
    )
```

```python
import functools

import jax
import jax.numpy as jnp
from jax import lax
from jax.experimental import pallas as pl
from jax.experimental.pallas import tpu as pltpu
from jax.sharding import PartitionSpec as P

F32 = jnp.float32
BF16 = jnp.bfloat16
MESH = pl.DeviceIdType.MESH


def shards(
    tokens,
    routes,
    route_weight,
    gate_first,
    up_first,
    gate_second,
    up_second,
    down_first,
    down_second,
):
    tok_rows, width_here = tokens.shape
    top_k = routes.shape[1]
    groups = lax.axis_size("expert")
    dp_count = lax.axis_size("dp")
    per_dev, blocks_here, block_width, rank_size = gate_first.shape
    rank_here = gate_second.shape[1]
    block_count = gate_second.shape[2]
    experts = per_dev * groups
    capacity = 2 * tok_rows * top_k // experts
    flat_routes = routes.reshape(-1)
    pair_count = flat_routes.shape[0]
    one_hot = (flat_routes[:, None] == jnp.arange(experts, dtype=jnp.int32)[None, :]).astype(
        jnp.int32
    )
    earlier = jnp.cumsum(one_hot, axis=0) - one_hot
    position = jnp.sum(earlier * one_hot, axis=1)
    counts = jnp.sum(one_hot, axis=0)
    slot_index = flat_routes * capacity + position
    pair_token = jnp.arange(pair_count, dtype=jnp.int32) // top_k
    slot_token = jnp.full((experts * capacity,), tok_rows, jnp.int32).at[slot_index].set(pair_token)
    outgoing = jnp.take(tokens, slot_token, axis=0, mode="fill", fill_value=0).reshape(
        groups, per_dev, capacity, width_here
    )
    gate_wide = gate_second.reshape(per_dev, rank_here, dp_count, blocks_here, block_count)
    up_wide = up_second.reshape(per_dev, rank_here, dp_count, blocks_here, block_count)
    down_wide = down_second.reshape(per_dev, blocks_here, dp_count, rank_here, block_width)
    received = lax.all_to_all(outgoing, "expert", split_axis=0, concat_axis=0, tiled=True)
    sources = received.shape[0]
    local = received.shape[1]
    slots = received.shape[2]
    split_rows = received.reshape(sources, local, slots, blocks_here, block_width)
    gate_low = jnp.einsum(
        "aesbf,ebfr->rbeas", split_rows, gate_first, preferred_element_type=jnp.float32
    )
    up_low = jnp.einsum(
        "aesbf,ebfr->rbeas", split_rows, up_first, preferred_element_type=jnp.float32
    )
    layout = (dp_count, rank_here, blocks_here, local, sources, slots)
    gate_mixed = lax.all_to_all(
        gate_low.astype(jnp.bfloat16).reshape(layout), "dp", split_axis=0, concat_axis=0, tiled=True
    )
    up_mixed = lax.all_to_all(
        up_low.astype(jnp.bfloat16).reshape(layout), "dp", split_axis=0, concat_axis=0, tiled=True
    )
    gate_high = jnp.einsum(
        "qcjeas,ecqjm->ecmas", gate_mixed, gate_wide, preferred_element_type=jnp.float32
    )
    up_high = jnp.einsum(
        "qcjeas,ecqjm->ecmas", up_mixed, up_wide, preferred_element_type=jnp.float32
    )
    activated = (jax.nn.silu(gate_high) * up_high).astype(jnp.bfloat16)
    down_low = jnp.einsum(
        "ecmas,ecmn->ecnas", activated, down_first, preferred_element_type=jnp.float32
    )
    down_split = down_low.astype(jnp.bfloat16).reshape(
        local, rank_here, dp_count, blocks_here, sources, slots
    )
    down_mixed = lax.all_to_all(down_split, "dp", split_axis=2, concat_axis=2, tiled=True)
    expert_out = jnp.einsum(
        "ecqjas,ejqcf->aesjf", down_mixed, down_wide, preferred_element_type=jnp.float32
    )
    result = expert_out.astype(jnp.bfloat16).reshape(sources, local, slots, width_here)
    totals = lax.psum(counts, "expert")
    own_counts = lax.dynamic_slice_in_dim(
        totals, lax.axis_index("expert") * per_dev, per_dev
    ).astype(jnp.float32)
    returned = lax.all_to_all(result, "expert", split_axis=0, concat_axis=0, tiled=True).reshape(
        experts * capacity, width_here
    )
    picked = jnp.take(returned, slot_index, axis=0).astype(jnp.float32)
    weighted = picked * route_weight.reshape(-1)[:, None]
    moe_output = jnp.sum(weighted.reshape(tok_rows, top_k, width_here), axis=1).astype(jnp.bfloat16)
    expert_load = own_counts * experts / (tok_rows * groups * top_k)
    return (moe_output, expert_load)


def xor(a, b, count):
    total, bit = 0, 1
    while bit < count:
        total = total + bit * ((a // bit + b // bit) % 2)
        bit *= 2
    return total


def dot(a, b):
    return jnp.dot(a, b, preferred_element_type=F32)


def ones_at(shape, row_to_column):
    lead = shape[:-1]
    target = row_to_column(*[lax.broadcasted_iota(jnp.int32, shape, d) for d in range(len(lead))])
    column = lax.broadcasted_iota(jnp.int32, shape, len(lead))
    hit = jnp.where(column == target, F32(1), F32(0))
    return hit.reshape(-1, shape[-1]).astype(BF16)


def expert_kernel(
    sizes,
    tok, routes, shares_in, gf, uf, gs, df, ds,
    out, load,
    tok_all, routes_all, shares_all, gf2, uf2, gs2, df2, ds2,
    w1, w2, w3, w4, wide, rows, low_out, low_in, down_out, down_in,
    combine, made, summed, z_out, z_in, counts, counts_in,
    gather_s, gather_r, weight_s, weight_r, low_s, low_r, down_s, down_r,
    local_s, count_s, z_s, z_r,
):
    groups, dp, top_k, cap, rank_here, block_count = sizes
    per_dev, blocks, rank, width = gf.shape
    tok_rows, features = tok.shape
    experts = per_dev * groups
    half = blocks // 2
    half_width = half * width
    chunk = 2 * rank_here * half
    pieces = 2 * dp
    hidden = rank_here * block_count
    nz = groups // 2
    total_steps = 2 * nz
    d = lax.axis_index("dp")
    g = lax.axis_index("expert")
    z, x = g // 2, g % 2
    partner = (d, z * 2 + (1 - x))

    def at_dp(r):
        return (xor(d, r, dp), g)

    def at_z(k):
        return (d, xor(z, k, nz) * 2 + x)

    def remote(src, dst, send, recv, to):
        return pltpu.make_async_remote_copy(
            src_ref=src, dst_ref=dst, send_sem=send, recv_sem=recv,
            device_id=to, device_id_type=MESH,
        )

    barrier = pltpu.get_barrier_semaphore()
    peers = [at_dp(r) for r in range(1, dp)] + [partner] + [at_z(k) for k in range(1, nz)]
    for peer in peers:
        pl.semaphore_signal(barrier, inc=1, device_id=peer, device_id_type=MESH)
    pl.semaphore_wait(barrier, len(peers))

    def gather(k):
        pairs = ((routes, routes_all), (shares_in, shares_all), (tok, tok_all))
        return [
            remote(src, dst.at[k], gather_s.at[n, k], gather_r.at[n, k], at_z(k))
            for n, (src, dst) in enumerate(pairs)
        ]

    held = (gf, uf, gs, df, ds)
    swapped = (gf2, uf2, gs2, df2, ds2)

    def swap(n):
        return remote(held[n], swapped[n], weight_s.at[n], weight_r.at[n], partner)

    for k in range(1, nz):
        for copy in gather(k):
            copy.start()
    for n in range(len(held)):
        swap(n).start()
    tok_all[0] = tok[...]
    routes_all[0] = routes[...]
    shares_all[0] = shares_in[...]
    counts[...] = jnp.zeros_like(counts)

    def spread_first(gate, up):
        @pl.loop(0, blocks)
        def _(b):
            j = b % half
            place = ones_at(
                (2, dp, rank_here, dp * chunk),
                lambda side, q, c: q * chunk + side * (chunk // 2) + c * half + j,
            )
            for e in range(per_dev):
                both = jnp.concatenate([gate[e, b], up[e, b]], axis=0)
                w1[e, b] = lax.dot_general(
                    both, place, (((0,), (0,)), ((), ())), preferred_element_type=F32
                ).astype(BF16)

    def spread_middle(second, third):
        wide[...] = jnp.zeros_like(wide)
        lanes = sorted({(c * block_count) % 128 for c in range(rank_here)})
        places = {
            (side, lane): ones_at(
                (2, block_count, 128), lambda s, r: jnp.where(s == side, r + lane, -1)
            )
            for side in range(2)
            for lane in lanes
        }

        @pl.loop(0, per_dev)
        def _(e):
            for side in range(2):
                for c in range(rank_here):
                    lane = (c * block_count) % 128
                    value = dot(second[e, c], places[side, lane])
                    row = side * (chunk // 2) + c * half
                    start = side * hidden + c * block_count - lane
                    wide[:, row : row + half, start : start + 128] = value.reshape(
                        pieces, half, 128
                    )
            for piece in range(pieces):
                w2[e, piece] = wide[piece].astype(BF16)

        @pl.loop(0, rank_here)
        def _(c):
            pairs = rank_here // 2
            place = ones_at(
                (2, block_count, hidden),
                lambda s, r: jnp.where(s == c // pairs, r * rank_here + c, -1),
            )
            value = dot(third[:, c % pairs].reshape(-1, 2 * block_count), place)
            w3[:, c] = value.astype(BF16).reshape(per_dev, block_count, hidden)

    def spread_last(fourth):
        wide[...] = jnp.zeros_like(wide)
        places = {}
        for j in range(half):
            lane = (j * width) % 128
            span = -(-(lane + width) // 128) * 128
            places[j] = ones_at((width, span), lambda r: r + lane)

        @pl.loop(0, per_dev)
        def _(e):
            for n in range(blocks):
                h = n // half
                offset = (n % half) * width
                lane = offset % 128
                span = -(-(lane + width) // 128) * 128
                value = dot(fourth[e, n], places[n % half])
                wide[
                    h * dp : (h + 1) * dp,
                    n * rank_here : (n + 1) * rank_here,
                    offset - lane : offset - lane + span,
                ] = value.reshape(dp, rank_here, span)
            for q in range(dp):
                for h in range(2):
                    w4[e, q, :, h * half_width : (h + 1) * half_width] = wide[
                        h * dp + q, :, :half_width
                    ].astype(BF16)

    def place_of(i):
        turn = i // nz
        return turn, (i % nz) * (1 - turn) + (nz - 1 - i % nz) * turn

    def low_copy(i, r):
        return remote(
            low_out.at[i % 2, xor(d, r, dp)], low_in.at[i, d],
            low_s.at[i % 2, r], low_r.at[i, r], at_dp(r),
        )

    def down_copy(i, r):
        return remote(
            down_out.at[i % 2, xor(d, r, dp)], down_in.at[i, d],
            down_s.at[i % 2, r], down_r.at[i, r], at_dp(r),
        )

    def low_local(i):
        return pltpu.make_async_copy(low_out.at[i % 2, d], low_in.at[i, d], local_s.at[0])

    def down_local(i):
        return pltpu.make_async_copy(down_out.at[i % 2, d], down_in.at[i, d], local_s.at[1])

    crossing = list(range(dp - 1, 0, -1))

    def stage_a(i):
        turn, k = place_of(i)

        @pl.when((turn == 0) & (k > 0))
        def _():
            for copy in gather(k):
                copy.wait_recv()

        @pl.when(i >= 2)
        def _():
            for r in crossing:
                low_copy(i, r).wait_send()

        base = (z * 2 + (x + turn) % 2) * per_dev
        named_rows, weights = routes_all[k], shares_all[k]
        line = lax.broadcasted_iota(jnp.int32, (8, tok_rows), 0)
        hits = jnp.zeros((8, tok_rows), F32)
        shares = []
        for e in range(per_dev):
            named = named_rows == base + e
            hit = jnp.max(jnp.where(named, F32(1), F32(0)), axis=0, keepdims=True)
            hits = hits + jnp.where(line == e, hit, F32(0))
            shares.append(jnp.sum(jnp.where(named, weights, F32(0)), axis=0, keepdims=True))
        counts[turn] += hits
        before = lax.broadcasted_iota(jnp.int32, (tok_rows, tok_rows), 0)
        after = lax.broadcasted_iota(jnp.int32, (tok_rows, tok_rows), 1)
        ahead = jnp.where(before < after, F32(1), F32(0)).astype(BF16)
        position = dot(hits.astype(BF16), ahead)
        position = jnp.where(hits > 0, position, F32(-1)).astype(jnp.int32)
        slot_row = lax.broadcasted_iota(jnp.int32, (cap, tok_rows), 0)
        pick, mix = [], []
        for e in range(per_dev):
            chosen = slot_row == position[e : e + 1]
            pick.append(jnp.where(chosen, F32(1), F32(0)))
            mix.append(jnp.where(chosen, shares[e], F32(0)))
        pick = jnp.concatenate(pick, axis=0).astype(BF16)
        combine[i] = jnp.concatenate(mix, axis=0).T.astype(BF16)
        rows[...] = dot(pick, tok_all[k]).astype(BF16)
        for e in range(per_dev):
            span = slice(e * cap, (e + 1) * cap)
            for h in range(2):
                weight = w1[e, h * half : (h + 1) * half].reshape(half_width, dp * chunk)
                low = dot(rows[span, h * half_width : (h + 1) * half_width], weight).astype(BF16)
                for q in range(dp):
                    low_out[i % 2, q, h, span, :] = low[:, q * chunk : (q + 1) * chunk]
        for r in crossing:
            low_copy(i, r).start()
        low_local(i).start()
        low_local(i).wait()

    def stage_b(i):
        for r in crossing:
            low_copy(i, r).wait_recv()

        @pl.when(i >= 2)
        def _():
            for r in crossing:
                down_copy(i, r).wait_send()

        for e in range(per_dev):
            span = slice(e * cap, (e + 1) * cap)
            low = jnp.concatenate(
                [low_in[i, p, h, span, :] for p in range(dp) for h in range(2)], axis=1
            )
            high = dot(low, w2[e].reshape(pieces * chunk, 2 * hidden))
            gate, up = high[:, :hidden], high[:, hidden:]
            activated = (gate / (1 + jnp.exp(-gate)) * up).astype(BF16)
            down = dot(activated, w3[e].reshape(hidden, hidden)).astype(BF16)
            for p in range(dp):
                down_out[i % 2, p, span, :] = down[:, p * chunk : (p + 1) * chunk]
        for r in crossing:
            down_copy(i, r).start()
        down_local(i).start()
        down_local(i).wait()

    def z_part(k):
        return remote(z_out.at[k], z_in.at[k], z_s.at[k], z_r.at[k], at_z(k))

    def stage_c(i):
        turn, k = place_of(i)
        for r in crossing:
            down_copy(i, r).wait_recv()
        for e in range(per_dev):
            span = slice(e * cap, (e + 1) * cap)
            down = jnp.concatenate([down_in[i, q, span, :] for q in range(dp)], axis=1)
            made[span, :] = dot(down, w4[e].reshape(dp * chunk, features)).astype(BF16)
        part = dot(combine[i], made[...])

        @pl.when(turn == 0)
        def _():
            summed[k] = part

        @pl.when((turn == 1) & (k == 0))
        def _():
            summed[k] += part

        @pl.when((turn == 1) & (k > 0))
        def _():
            z_out[k] = (summed[k] + part).astype(BF16)
            z_part(k).start()

    count_copy = remote(counts.at[1], counts_in, count_s.at[0], count_s.at[1], partner)

    spread_first(gf, uf)

    @pl.loop(0, total_steps + 2)
    def _(step):
        @pl.when(step == nz)
        def _():
            swap(0).wait_recv()
            swap(1).wait_recv()
            spread_first(gf2, uf2)

        @pl.when(step < total_steps)
        def _():
            stage_a(step)

        @pl.when(step == 0)
        def _():
            spread_middle(gs, df)
            spread_last(ds)

        @pl.when(step == total_steps)
        def _():
            count_copy.start()

        @pl.when(step == nz + 1)
        def _():
            swap(2).wait_recv()
            swap(3).wait_recv()
            spread_middle(gs2, df2)

        @pl.when((step >= 1) & (step <= total_steps))
        def _():
            stage_b(step - 1)

        @pl.when(step == nz + 2)
        def _():
            swap(4).wait_recv()
            spread_last(ds2)

        @pl.when(step >= 2)
        def _():
            stage_c(step - 2)

    count_copy.wait()
    ones = jnp.ones((8, tok_rows), BF16)
    held_rows = lax.dot_general(
        ones, (counts[0] + counts_in[...]).astype(BF16),
        (((1,), (1,)), ((), ())), preferred_element_type=F32,
    )
    load[...] = held_rows[:1, :per_dev] * experts / (tok_rows * groups * top_k)

    total = summed[0]
    for k in range(1, nz):
        z_part(k).wait_recv()
        total += z_in[k].astype(F32)
    out[...] = total.astype(BF16)

    for k in range(1, nz):
        for copy in gather(k):
            copy.wait_send()
        z_part(k).wait_send()
    for n in range(len(held)):
        swap(n).wait_send()
    for i in (total_steps - 2, total_steps - 1):
        for r in crossing:
            low_copy(i, r).wait_send()
            down_copy(i, r).wait_send()


def fused(
    tokens, routes, route_weight,
    gate_first, up_first, gate_second, up_second, down_first, down_second,
):
    tok_rows, features = tokens.shape
    top_k = routes.shape[1]
    groups = lax.axis_size("expert")
    dp = lax.axis_size("dp")
    per_dev, blocks, width, rank = gate_first.shape
    rank_here, block_count = gate_second.shape[1:3]
    experts = per_dev * groups
    cap = 2 * tok_rows * top_k // experts
    nz = groups // 2
    steps = 2 * nz
    chunk = 2 * rank_here * (blocks // 2)
    hidden = rank_here * block_count
    slots = per_dev * cap
    pairs = rank_here // 2
    factors = (
        gate_first.swapaxes(2, 3),
        up_first.swapaxes(2, 3),
        jnp.concatenate([gate_second, up_second], axis=3),
        jnp.concatenate([down_first[:, :pairs], down_first[:, pairs:]], axis=3),
        down_second,
    )
    vmem = pl.BlockSpec(memory_space=pltpu.VMEM)
    dma = pltpu.SemaphoreType.DMA
    out, load = pl.pallas_call(
        functools.partial(expert_kernel, (groups, dp, top_k, cap, rank_here, block_count)),
        out_shape=(
            jax.ShapeDtypeStruct((tok_rows, features), BF16),
            jax.ShapeDtypeStruct((1, per_dev), F32),
        ),
        in_specs=[vmem] * 8,
        out_specs=(vmem, vmem),
        scratch_shapes=[
            pltpu.VMEM((nz, tok_rows, features), BF16),
            pltpu.VMEM((nz, top_k, tok_rows), jnp.int32),
            pltpu.VMEM((nz, top_k, tok_rows), F32),
            *[pltpu.VMEM(factor.shape, BF16) for factor in factors],
            pltpu.VMEM((per_dev, blocks, width, dp * chunk), BF16),
            pltpu.VMEM((per_dev, 2 * dp, chunk, 2 * hidden), BF16),
            pltpu.VMEM((per_dev, rank_here, block_count, hidden), BF16),
            pltpu.VMEM((per_dev, dp, chunk, features), BF16),
            pltpu.VMEM((2 * dp, chunk, 2 * hidden), F32),
            pltpu.VMEM((slots, features), BF16),
            pltpu.VMEM((2, dp, 2, slots, chunk), BF16),
            pltpu.VMEM((steps, dp, 2, slots, chunk), BF16),
            pltpu.VMEM((2, dp, slots, chunk), BF16),
            pltpu.VMEM((steps, dp, slots, chunk), BF16),
            pltpu.VMEM((steps, tok_rows, slots), BF16),
            pltpu.VMEM((slots, features), BF16),
            pltpu.VMEM((nz, tok_rows, features), F32),
            pltpu.VMEM((nz, tok_rows, features), BF16),
            pltpu.VMEM((nz, tok_rows, features), BF16),
            pltpu.VMEM((2, 8, tok_rows), F32),
            pltpu.VMEM((8, tok_rows), F32),
            dma((3, nz)), dma((3, nz)), dma((5,)), dma((5,)),
            dma((2, dp)), dma((steps, dp)), dma((2, dp)), dma((steps, dp)),
            dma((2,)), dma((2,)), dma((nz,)), dma((nz,)),
        ],
        compiler_params=pltpu.CompilerParams(
            collective_id=0, has_side_effects=True, vmem_limit_bytes=67043328
        ),
    )(tokens, routes.T, route_weight.T, *factors)
    return (out, load.reshape(per_dev))


def chosen_plan(tokens, routes, route_weight, *weights):
    groups = lax.axis_size("expert")
    dp = lax.axis_size("dp")
    blocks, width = weights[0].shape[1:3]
    rank_here, block_count = weights[2].shape[1:3]
    tiled = (
        tokens.shape[0] % 128 == 0
        and 2 * rank_here * (blocks // 2) == 128
        and rank_here == 8
        and weights[0].shape[0] <= 8
        and blocks // 2 == 8
        and block_count == 2 * dp * 8
        and (blocks // 2 * width) % 128 == 0
    )
    powers = groups & (groups - 1) == 0 and dp & (dp - 1) == 0
    if groups <= 2 * routes.shape[1] and groups >= 4 and dp >= 2 and powers and tiled:
        return fused(tokens, routes, route_weight, *weights)
    return shards(tokens, routes, route_weight, *weights)


def solution(mesh):
    return jax.shard_map(
        chosen_plan,
        mesh=mesh,
        in_specs=(
            P("expert", "dp"),
            P("expert", None),
            P("expert", None),
            P("expert", "dp", None, None),
            P("expert", "dp", None, None),
            P("expert", "dp", None, None),
            P("expert", "dp", None, None),
            P("expert", "dp", None, None),
            P("expert", "dp", None, None),
        ),
        out_specs=(P("expert", "dp"), P("expert")),
        check_vma=False,
    )
```
